32 devices in a mesh: group: 2 (over y), seq: 4 (over z), doc: 4 (over x, core).
Axes of the slice: x: 2, y: 2, z: 4, core: 2. Of those that a mesh axis runs over, the one named last changes fastest.
Arguments:
- query_vectors: bfloat16 [8, 512, 1024], P(('group', 'doc'), 'seq'), parts along dimension 0, may hold values from -6 to 6
- key_vectors: bfloat16 [8, 512, 1024], P(('group', 'doc'), 'seq'), parts along dimension 0, may hold values from -6 to 6
- value_vectors: bfloat16 [8, 512, 1024], P(('group', 'doc'), 'seq'), parts along dimension 0, may hold values from -6 to 6
- out_grad: bfloat16 [8, 512, 1024], P(('group', 'doc'), 'seq'), parts along dimension 0, may hold values from -6 to 6
- pad_length: int32 [8], P(('group', 'doc')), parts along dimension 0, may hold values from 1 to 256
Outputs:
- attended: bfloat16 [8, 512, 1024], P(('group', 'doc'), 'seq'), parts along dimension 0
- query_grad: bfloat16 [8, 512, 1024], P(('group', 'doc'), 'seq'), parts along dimension 0
- key_grad: bfloat16 [8, 512, 1024], P(('group', 'doc'), 'seq'), parts along dimension 0
- value_grad: bfloat16 [8, 512, 1024], P(('group', 'doc'), 'seq'), parts along dimension 0
The draws below stay inside these ranges and needn't reach their ends.
There are 2 independent parts, one for each index of `group`. The reference program is written for one: setup_inputs(seed, part) draws one part's arguments, and reference() takes and returns one part's arrays. A program takes and returns all parts, laid end to end along the dimension named above; each array names one. Nothing has to cross between parts.
All inputs are finite; a program needn't handle non-finite values.
Results may differ from the reference program's by a relative error of at most 0.015.
Values may be sent and summed in bfloat16 or wider, within the bound.
A program may use at most 64 MiB of HBM per device.

```python
import math
import jax
import jax.numpy as jnp
from jax import lax

D = 1024
H = 16
W = 128
G = 64
TOK_DEV = 128
DOCS = 4
LENGTH = 512


def draw_query_vectors(key, part):
    result = jnp.clip(jax.random.normal(jax.random.fold_in(key, 1), (DOCS, LENGTH, D), jnp.float32), -6.0, 6.0)
    return result.astype(jnp.bfloat16)


def draw_key_vectors(key, part):
    result = jnp.clip(jax.random.normal(jax.random.fold_in(key, 3), (DOCS, LENGTH, D), jnp.float32), -6.0, 6.0)
    return result.astype(jnp.bfloat16)


def touch_ends(entries, key, low, top_value):
    dims = entries.shape
    index_at = [jax.random.randint(jax.random.fold_in(key, axis), (), 0, dims[axis]) for axis in range(len(dims))]
    entries = entries.at[tuple(index_at)].set(low)
    longest = dims.index(max(dims))
    index_at[longest] = (index_at[longest] + 1) % dims[longest]
    return entries.at[tuple(index_at)].set(top_value)


def steps_of(stream_key, shape, split, least, high):
    level = 1.0
    for position, shards_of in split:
        heights = jax.random.uniform(jax.random.fold_in(jax.random.fold_in(stream_key, 6), position), (shards_of,), jnp.float32, least / len(split), high / len(split))
        level = level * jnp.repeat(jnp.exp(heights), shape[position] // shards_of).reshape((-1,) + (1,) * (len(shape) - 1 - position))
    return level


def scatter_about(own_key, extent, scale, most, shards=(), kind=jnp.bfloat16):
    loudness = steps_of(own_key, extent, shards, -0.22, 0.18) if shards else 1.0
    drawn = jax.random.normal(own_key, extent, jnp.float32) * scale * loudness
    return jnp.minimum(jnp.maximum(drawn, -most), most).astype(kind)


def setup_inputs(seed: int = 0, part: int = 0) -> dict:
    arg_keys = jax.random.split(jax.random.key(seed), 6)
    part_splits = jax.random.split(jax.random.fold_in(arg_keys[5], part), 6)
    query_vectors = draw_query_vectors(jax.random.fold_in(jax.random.fold_in(arg_keys[5], part), 71), part)
    key_vectors = draw_key_vectors(jax.random.fold_in(jax.random.fold_in(arg_keys[5], part), 71), part)
    value_vectors = scatter_about(part_splits[2], (DOCS, LENGTH, D), 1.0, 6.0, ((0, 4), (1, 4)))
    out_grad = scatter_about(part_splits[3], (DOCS, LENGTH, D), 1.0, 6.0, ((0, 4), (1, 4)))
    pad_length = touch_ends(jax.random.randint(part_splits[4], (DOCS,), 1, 2 * TOK_DEV + 1), jax.random.fold_in(part_splits[4], 1), 1, 2 * TOK_DEV).astype(jnp.int32)
    return {"query_vectors": query_vectors, "key_vectors": key_vectors, "value_vectors": value_vectors, "out_grad": out_grad, "pad_length": pad_length}


very_negative = -1e+30

def split_heads(block_rows):
    return block_rows.reshape(block_rows.shape[0], H, D // H)

def join_heads(block_rows):
    return block_rows.reshape(block_rows.shape[0], D)

def product(form, left_side, right_side):
    return jnp.einsum(form, left_side.astype(jnp.float32), right_side.astype(jnp.float32), precision=lax.Precision.HIGHEST)

def band_terms(query_rows, grad_rows, key_all, value_all, allowed, row_live):
    score_scale = 1.0 / math.sqrt(D // H)
    query_heads = split_heads(query_rows)
    grad_heads = split_heads(grad_rows)
    key_heads = split_heads(key_all)
    value_heads = split_heads(value_all)
    scores = product('qhd,khd->hqk', query_heads, key_heads) * score_scale
    scores = jnp.where(allowed[None], scores, very_negative)
    largest = lax.optimization_barrier(jnp.max(scores, axis=2, keepdims=True))
    expo = jnp.where(allowed[None], jnp.exp(scores - largest), 0.0)
    totals = lax.optimization_barrier(jnp.sum(expo, axis=2, keepdims=True))
    probs = expo / totals
    probs_low = probs.astype(jnp.bfloat16)
    attn = product('hqk,khd->qhd', probs_low, value_heads)
    delta = lax.optimization_barrier(jnp.sum(grad_heads.astype(jnp.float32) * attn, axis=2)).T
    dprob = product('qhd,khd->hqk', grad_heads, value_heads)
    keep_rows = row_live[None, :, None]
    dscore = jnp.where(keep_rows, probs * (dprob - delta[:, :, None]), 0.0).astype(jnp.bfloat16)
    kept_low = jnp.where(keep_rows, probs_low, jnp.zeros_like(probs_low))
    query_grad = product('hqk,khd->qhd', dscore, key_heads) * score_scale
    key_grad = product('hqk,qhd->khd', dscore, query_heads) * score_scale
    value_grad = product('hqk,qhd->khd', kept_low, grad_heads)
    return (join_heads(attn), join_heads(query_grad), join_heads(key_grad), join_heads(value_grad))

def one_doc(doc_inputs):
    query_doc, key_doc, value_doc, grad_doc, pad_count = doc_inputs
    doc_length = query_doc.shape[0]
    block_rows = TOK_DEV
    block_count = doc_length // block_rows
    score_scale = 1.0 / math.sqrt(D // H)
    suffix_start = doc_length - G
    valid_end = suffix_start - pad_count
    query_glob = query_doc[suffix_start:]
    key_glob = key_doc[suffix_start:]
    value_glob = value_doc[suffix_start:]
    grad_glob = grad_doc[suffix_start:]
    key_padded = jnp.pad(key_doc, ((W, W), (0, 0)))
    value_padded = jnp.pad(value_doc, ((W, W), (0, 0)))

    def one_block(block_index):
        first_row = block_index * block_rows
        query_pos = first_row + jnp.arange(block_rows, dtype=jnp.int32)
        window_pos = first_row - W + jnp.arange(block_rows + 2 * W, dtype=jnp.int32)
        query_rows = lax.dynamic_slice_in_dim(query_doc, first_row, block_rows, 0)
        grad_rows = lax.dynamic_slice_in_dim(grad_doc, first_row, block_rows, 0)
        key_window = lax.dynamic_slice_in_dim(key_padded, first_row, block_rows + 2 * W, 0)
        value_window = lax.dynamic_slice_in_dim(value_padded, first_row, block_rows + 2 * W, 0)
        within = (jnp.abs(query_pos[:, None] - window_pos[None, :]) <= W) & (window_pos >= 0)[None, :] & (window_pos < valid_end)[None, :]
        allowed = jnp.concatenate([within, jnp.ones((block_rows, G), dtype=bool)], axis=1)
        key_all = jnp.concatenate([key_window, key_glob], axis=0)
        value_all = jnp.concatenate([value_window, value_glob], axis=0)
        return band_terms(query_rows, grad_rows, key_all, value_all, allowed, query_pos < suffix_start)
    attn_all, qgrad_all, kgrad_all, vgrad_all = lax.map(one_block, jnp.arange(block_count, dtype=jnp.int32))
    attn_band = attn_all.reshape(doc_length, D)
    query_band = qgrad_all.reshape(doc_length, D)

    def gather_band(grad_all):
        middle = grad_all[:, W:W + block_rows]
        middle = middle.at[:-1, block_rows - W:].add(grad_all[1:, :W])
        middle = middle.at[1:, :W].add(grad_all[:-1, W + block_rows:2 * W + block_rows])
        return (middle.reshape(doc_length, D), lax.optimization_barrier(jnp.sum(grad_all[:, 2 * W + block_rows:], axis=0)))
    key_band, key_suffix = gather_band(kgrad_all)
    value_band, value_suffix = gather_band(vgrad_all)
    positions = jnp.arange(doc_length, dtype=jnp.int32)
    local_live = (positions < valid_end) | (positions >= suffix_start)
    query_gh = split_heads(query_glob)
    grad_gh = split_heads(grad_glob)
    key_heads = split_heads(key_doc)
    value_heads = split_heads(value_doc)
    gscores = product('ghd,khd->hgk', query_gh, key_heads) * score_scale
    gscores = jnp.where(local_live[None, None, :], gscores, very_negative)
    largest = lax.optimization_barrier(jnp.max(gscores, axis=2, keepdims=True))
    expo = jnp.where(local_live[None, None, :], jnp.exp(gscores - largest), 0.0)
    gprobs = expo / lax.optimization_barrier(jnp.sum(expo, axis=2, keepdims=True))
    gprobs_low = gprobs.astype(jnp.bfloat16)
    attn_glob = product('hgk,khd->ghd', gprobs_low, value_heads)
    delta_glob = lax.optimization_barrier(jnp.sum(grad_gh.astype(jnp.float32) * attn_glob, axis=2)).T
    gdprob = product('ghd,khd->hgk', grad_gh, value_heads)
    gdscore = (gprobs * (gdprob - delta_glob[:, :, None])).astype(jnp.bfloat16)
    query_suffix = join_heads(product('hgk,khd->ghd', gdscore, key_heads)) * score_scale
    key_add = join_heads(product('hgk,ghd->khd', gdscore, query_gh)) * score_scale
    value_add = join_heads(product('hgk,ghd->khd', gprobs_low, grad_gh))
    attended = attn_band.at[suffix_start:].set(join_heads(attn_glob))
    query_grad = query_band.at[suffix_start:].add(query_suffix)
    key_grad = (key_band + key_add).at[suffix_start:].add(key_suffix)
    value_grad = (value_band + value_add).at[suffix_start:].add(value_suffix)
    return (attended.astype(jnp.bfloat16), query_grad.astype(jnp.bfloat16), key_grad.astype(jnp.bfloat16), value_grad.astype(jnp.bfloat16))

def reference(query_vectors, key_vectors, value_vectors, out_grad, pad_length):
    attended, query_grad, key_grad, value_grad = lax.map(one_doc, (query_vectors, key_vectors, value_vectors, out_grad, pad_length))
    return (attended, query_grad, key_grad, value_grad)
```

```python
import functools
import math

import jax
import jax.numpy as jnp
from jax import lax
from jax.experimental import pallas as pl
from jax.experimental.pallas import tpu as pltpu
from jax.sharding import PartitionSpec as P

D = 1024
H = 16
W = 128
G = 64
HEAD = D // H
PAIR = 2 * HEAD

MESH = pl.DeviceIdType.MESH
very_negative = -1e30
scale = 1.0 / math.sqrt(HEAD)
f32 = jnp.float32
bf16 = jnp.bfloat16


def dot_nt(a, b):
    return lax.dot_general(a, b, (((1,), (1,)), ((), ())), preferred_element_type=f32)


def dot_nn(a, b):
    return lax.dot_general(a, b, (((1,), (0,)), ((), ())), preferred_element_type=f32)


def dot_tn(a, b):
    return lax.dot_general(a, b, (((0,), (0,)), ((), ())), preferred_element_type=f32)


def iota(shape, dim):
    return lax.broadcasted_iota(jnp.int32, shape, dim)


def pair_mask(value):
    lane = iota((1, PAIR), 1)
    first = jnp.where(lane < HEAD, value, 0.0).astype(bf16)
    second = jnp.where(lane < HEAD, 0.0, value).astype(bf16)
    return first, second


def two_heads(rows, value):
    first, second = pair_mask(value)
    return jnp.concatenate([rows * first, rows * second], axis=0)


def one_pair(stacked):
    half = stacked.shape[0] // 2
    lane = iota((half, PAIR), 1)
    return jnp.where(lane < HEAD, stacked[:half], stacked[half:])


def kernel(
    n, rows, chunks,
    pad_ref, q_ref, k_ref, v_ref, g_ref,
    att_ref, qgrad_ref, kgrad_ref, vgrad_ref,
    kv, qg, stats, bias, key_bias, expo_s, dprob_s,
    own_grad, suf_grad, down_out, down_in, up_out, up_in, chain_out, chain_in,
    qg_send, qg_recv, suf_send, suf_recv, low_send, low_recv, high_send, high_recv,
    stat_send, stat_recv, down_send, down_recv, up_send, up_recv, chain_send, chain_recv,
):
    me = lax.axis_index("seq")
    last = n - 1
    below = lax.rem(me + n - 1, n)
    above = lax.rem(me + 1, n)
    has_below = me > 0
    has_above = me < last
    all_keys = rows + 2 * W + G
    own = slice(W, W + rows)
    low = slice(0, W)
    high = slice(W + rows, 2 * W + rows)
    suf = slice(2 * W + rows, all_keys)
    tail = slice(rows - G, rows)

    def remote(src, dst, send, recv, target):
        return pltpu.make_async_remote_copy(
            src_ref=src, dst_ref=dst, send_sem=send, recv_sem=recv,
            device_id={"seq": target}, device_id_type=MESH,
        )

    def send_qg(c):
        return remote(qg.at[c], qg.at[c], qg_send.at[c], qg_recv.at[c], below)

    def send_suf(c):
        return remote(kv.at[c, :, suf], kv.at[c, :, suf], suf_send.at[c], suf_recv.at[c], below)

    def send_low(c):
        return remote(kv.at[c, :, own], kv.at[c, :, high], low_send.at[c], low_recv.at[c], below)

    def send_high(c):
        return remote(kv.at[c, :, own], kv.at[c, :, low], high_send.at[c], high_recv.at[c], above)

    def send_down(c):
        return remote(down_out.at[c], down_in.at[c], down_send.at[c], down_recv.at[c], below)

    def send_up(c):
        return remote(up_out.at[c], up_in.at[c], up_send.at[c], up_recv.at[c], above)

    def send_chain(c):
        return remote(chain_out.at[c], chain_in.at[c], chain_send.at[c], chain_recv.at[c], above)

    def send_stats(k):
        return remote(
            stats.at[0], stats.at[k], stat_send.at[k], stat_recv.at[k], lax.rem(me + k, n)
        )

    barrier = pltpu.get_barrier_semaphore()
    for k in range(1, n):
        pl.semaphore_signal(
            barrier, inc=1, device_id={"seq": lax.rem(me + k, n)}, device_id_type=MESH
        )

    for c in range(chunks):
        columns = slice(c * PAIR, (c + 1) * PAIR)
        kv[c, 0, own] = k_ref[:, columns]
        kv[c, 1, own] = v_ref[:, columns]

    @pl.when(me == last)
    def _():
        for c in range(chunks):
            columns = slice(c * PAIR, (c + 1) * PAIR)
            qg[c, 0] = q_ref[tail, columns]
            qg[c, 1] = g_ref[tail, columns]
            kv[c, 0, suf] = k_ref[tail, columns]
            kv[c, 1, suf] = v_ref[tail, columns]
            kv[c, :, high] = jnp.zeros((2, W, PAIR), bf16)

    @pl.when(me == 0)
    def _():
        for c in range(chunks):
            kv[c, :, low] = jnp.zeros((2, W, PAIR), bf16)

    pl.semaphore_wait(barrier, n - 1)

    @pl.when(has_above)
    def _():
        for c in range(chunks):
            send_high(c).start()

    @pl.when(me == last)
    def _():
        for c in range(chunks):
            send_qg(c).start()
        for c in range(chunks):
            send_suf(c).start()
            send_low(c).start()

    suffix_start = rows * n - G
    valid_end = suffix_start - pad_ref[0]
    first_row = me * rows
    j = iota((all_keys, 2 * rows), 0)
    i = iota((all_keys, 2 * rows), 1)
    i = jnp.where(i >= rows, i - rows, i)
    key_pos = first_row - W + j
    apart = i - (j - W)
    within = (apart <= W) & (apart >= -W) & (key_pos >= 0) & (key_pos < valid_end)
    bias[...] = jnp.where(within | (j >= 2 * W + rows), 0.0, very_negative)
    own_pos = first_row + iota((rows, 2 * G), 0)
    key_bias[...] = jnp.where(
        (own_pos < valid_end) | (own_pos >= suffix_start), 0.0, very_negative
    )
    query_lane = iota((1, 2 * rows), 1)
    query_pos = first_row + jnp.where(query_lane >= rows, query_lane - rows, query_lane)
    row_live = jnp.where(query_pos < suffix_start, 1.0, 0.0)

    def forward_stats(c, carry):
        @pl.when(has_above)
        def _():
            send_qg(c).wait_recv()

            @pl.when(has_below)
            def _():
                send_qg(c).start()

        query_two = two_heads(qg[c, 0], scale)
        grad_two = two_heads(qg[c, 1], 1.0)
        scores = dot_nt(kv[c, 0, own], query_two) + key_bias[...]
        largest = jnp.max(scores, axis=0, keepdims=True)
        expo = jnp.exp(scores - largest)
        dprob = dot_nt(kv[c, 1, own], grad_two)
        total = jnp.sum(expo, axis=0, keepdims=True)
        weighted = jnp.sum(expo * dprob, axis=0, keepdims=True)
        expo_s[c] = expo
        dprob_s[c] = dprob
        row = iota((8, 2 * G), 0)
        stats[0, c] = jnp.where(row == 0, largest, jnp.where(row == 1, total, weighted))
        return carry

    lax.fori_loop(0, chunks, forward_stats, 0)
    for k in range(1, n):
        send_stats(k).start()

    def band(c, carry):
        @pl.when(has_above)
        def _():
            send_suf(c).wait_recv()

            @pl.when(has_below)
            def _():
                send_suf(c).start()
                send_low(c).start()

        @pl.when(has_below)
        def _():
            send_high(c).wait_recv()

        @pl.when(has_above)
        def _():
            send_low(c).wait_recv()

        columns = pl.ds(pl.multiple_of(c * PAIR, PAIR), PAIR)
        query_two = two_heads(q_ref[:, columns], scale)
        grad_two = two_heads(g_ref[:, columns], 1.0)
        keys = kv[c, 0]
        values = kv[c, 1]
        scores = dot_nt(keys, query_two) + bias[...]
        largest = jnp.max(scores, axis=0, keepdims=True)
        expo = jnp.exp(scores - largest)
        total = jnp.sum(expo, axis=0, keepdims=True)
        dprob = dot_nt(values, grad_two)
        inverse = 1.0 / total
        delta = jnp.sum(expo * dprob, axis=0, keepdims=True) * inverse
        probs = expo * (inverse * row_live)
        probs_low = probs.astype(bf16)
        dscore = (probs * (dprob - delta)).astype(bf16)
        att_ref[:, columns] = one_pair(dot_tn(probs_low, values)).astype(bf16)
        qgrad_ref[:, columns] = (one_pair(dot_tn(dscore, keys)) * scale).astype(bf16)
        key_all = dot_nn(dscore, query_two)
        value_all = dot_nn(probs_low, grad_two)
        down_out[c, 0] = key_all[low].astype(bf16)
        down_out[c, 1] = value_all[low].astype(bf16)
        up_out[c, 0] = key_all[high].astype(bf16)
        up_out[c, 1] = value_all[high].astype(bf16)

        @pl.when(has_below)
        def _():
            send_down(c).start()

        @pl.when(has_above)
        def _():
            send_up(c).start()

        own_grad[c, 0] = key_all[own]
        own_grad[c, 1] = value_all[own]
        suf_grad[c, 0] = key_all[suf]
        suf_grad[c, 1] = value_all[suf]
        return carry


    lax.fori_loop(0, chunks, band, 0)

    for k in range(1, n):
        send_stats(k).wait_recv()

    def finish(c, carry):
        columns = pl.ds(pl.multiple_of(c * PAIR, PAIR), PAIR)
        parts = [stats[k, c] for k in range(n)]
        top = parts[0][0:1]
        for part in parts[1:]:
            top = jnp.maximum(top, part[0:1])
        factors = [jnp.exp(part[0:1] - top) for part in parts]
        total = sum(factor * part[1:2] for factor, part in zip(factors, parts))
        weighted = sum(factor * part[2:3] for factor, part in zip(factors, parts))
        inverse = 1.0 / total
        delta = weighted * inverse
        probs = expo_s[c] * (factors[0] * inverse)
        probs_low = probs.astype(bf16)
        dscore = (probs * (dprob_s[c] - delta)).astype(bf16)
        query_two = two_heads(qg[c, 0], scale)
        grad_two = two_heads(qg[c, 1], 1.0)
        att_part = one_pair(dot_tn(probs_low, kv[c, 1, own]))
        query_part = one_pair(dot_tn(dscore, kv[c, 0, own])) * scale
        suf_key = suf_grad[c, 0]
        suf_value = suf_grad[c, 1]
        key_sum = own_grad[c, 0] + dot_nn(dscore, query_two)
        value_sum = own_grad[c, 1] + dot_nn(probs_low, grad_two)

        @pl.when(me == 0)
        def _():
            chain_out[c, 0] = att_part.astype(bf16)
            chain_out[c, 1] = query_part.astype(bf16)
            chain_out[c, 2] = suf_key.astype(bf16)
            chain_out[c, 3] = suf_value.astype(bf16)

        own_grad[c, 0] = key_sum
        own_grad[c, 1] = value_sum

        @pl.when(has_below)
        def _():
            send_chain(c).wait_recv()
            att_sum = att_part + chain_in[c, 0].astype(f32)
            query_sum = query_part + chain_in[c, 1].astype(f32)
            key_suf = suf_key + chain_in[c, 2].astype(f32)
            value_suf = suf_value + chain_in[c, 3].astype(f32)

            @pl.when(has_above)
            def _():
                chain_out[c, 0] = att_sum.astype(bf16)
                chain_out[c, 1] = query_sum.astype(bf16)
                chain_out[c, 2] = key_suf.astype(bf16)
                chain_out[c, 3] = value_suf.astype(bf16)

            @pl.when(me == last)
            def _():
                att_ref[tail, columns] = att_sum.astype(bf16)
                qgrad_ref[tail, columns] = query_sum.astype(bf16)
                own_grad[c, 0, tail] = own_grad[c, 0, tail] + key_suf
                own_grad[c, 1, tail] = own_grad[c, 1, tail] + value_suf

        @pl.when(has_above)
        def _():
            send_chain(c).start()

        return carry

    lax.fori_loop(0, chunks, finish, 0)

    def combine(c, carry):
        columns = pl.ds(pl.multiple_of(c * PAIR, PAIR), PAIR)

        @pl.when(has_below)
        def _():
            send_up(c).wait_recv()
            own_grad[c, :, 0:W] = own_grad[c, :, 0:W] + up_in[c].astype(f32)

        @pl.when(has_above)
        def _():
            send_down(c).wait_recv()
            own_grad[c, :, rows - W : rows] = own_grad[c, :, rows - W : rows] + down_in[
                c
            ].astype(f32)

        kgrad_ref[:, columns] = own_grad[c, 0].astype(bf16)
        vgrad_ref[:, columns] = own_grad[c, 1].astype(bf16)
        return carry

    lax.fori_loop(0, chunks, combine, 0)

    def drain(c, carry):
        @pl.when(has_below)
        def _():
            send_qg(c).wait_send()
            send_suf(c).wait_send()
            send_low(c).wait_send()
            send_down(c).wait_send()

        @pl.when(has_above)
        def _():
            send_high(c).wait_send()
            send_up(c).wait_send()
            send_chain(c).wait_send()

        return carry

    lax.fori_loop(0, chunks, drain, 0)
    for k in range(1, n):
        send_stats(k).wait_send()


def per_device(n, query_vectors, key_vectors, value_vectors, out_grad, pad_length):
    rows, features = query_vectors.shape[1:]
    chunks = features // PAIR
    all_keys = rows + 2 * W + G
    vmem = pl.BlockSpec(memory_space=pltpu.VMEM)
    smem = pl.BlockSpec(memory_space=pltpu.SMEM)
    out = jax.ShapeDtypeStruct((rows, features), bf16)
    dma = pltpu.SemaphoreType.DMA
    outs = pl.pallas_call(
        functools.partial(kernel, n, rows, chunks),
        out_shape=(out,) * 4,
        in_specs=[smem] + [vmem] * 4,
        out_specs=(vmem,) * 4,
        scratch_shapes=[
            pltpu.VMEM((chunks, 2, all_keys, PAIR), bf16),
            pltpu.VMEM((chunks, 2, G, PAIR), bf16),
            pltpu.VMEM((n, chunks, 8, 2 * G), f32),
            pltpu.VMEM((all_keys, 2 * rows), f32),
            pltpu.VMEM((rows, 2 * G), f32),
            pltpu.VMEM((chunks, rows, 2 * G), f32),
            pltpu.VMEM((chunks, rows, 2 * G), f32),
            pltpu.VMEM((chunks, 2, rows, PAIR), f32),
            pltpu.VMEM((chunks, 2, G, PAIR), f32),
            pltpu.VMEM((chunks, 2, W, PAIR), bf16),
            pltpu.VMEM((chunks, 2, W, PAIR), bf16),
            pltpu.VMEM((chunks, 2, W, PAIR), bf16),
            pltpu.VMEM((chunks, 2, W, PAIR), bf16),
            pltpu.VMEM((chunks, 4, G, PAIR), bf16),
            pltpu.VMEM((chunks, 4, G, PAIR), bf16),
        ]
        + [dma((chunks,))] * 8
        + [dma((n,))] * 2
        + [dma((chunks,))] * 6,
        compiler_params=pltpu.CompilerParams(
            collective_id=0, has_side_effects=True, vmem_limit_bytes=48 << 20
        ),
    )(pad_length, query_vectors[0], key_vectors[0], value_vectors[0], out_grad[0])
    return tuple(array[None] for array in outs)


def solution(mesh):
    rows = P(("group", "doc"), "seq", None)
    return jax.shard_map(
        functools.partial(per_device, mesh.shape["seq"]),
        mesh=mesh,
        in_specs=(rows, rows, rows, rows, P(("group", "doc"))),
        out_specs=(rows,) * 4,
        check_vma=False,
    )
```

```python
import functools
import math

import jax
import jax.numpy as jnp
from jax import lax
from jax.experimental import pallas as pl
from jax.experimental.pallas import tpu as pltpu
from jax.sharding import PartitionSpec as P

D = 1024
H = 16
W = 128
G = 64
HEAD = D // H
PAIR = 2 * HEAD
AHEAD = 2
CHAIN_LAG = 3
UP_LAG = 2
DOWN_LAG = 2

MESH = pl.DeviceIdType.MESH
very_negative = -1e30
scale = 1.0 / math.sqrt(HEAD)
f32 = jnp.float32
bf16 = jnp.bfloat16


def dot_nt(a, b):
    return lax.dot_general(a, b, (((1,), (1,)), ((), ())), preferred_element_type=f32)


def dot_nn(a, b):
    return lax.dot_general(a, b, (((1,), (0,)), ((), ())), preferred_element_type=f32)


def dot_tn(a, b):
    return lax.dot_general(a, b, (((0,), (0,)), ((), ())), preferred_element_type=f32)


def iota(shape, dim):
    return lax.broadcasted_iota(jnp.int32, shape, dim)


def pair_mask(value):
    lane = iota((1, PAIR), 1)
    first = jnp.where(lane < HEAD, value, 0.0).astype(bf16)
    second = jnp.where(lane < HEAD, 0.0, value).astype(bf16)
    return first, second


def two_heads(rows, value):
    first, second = pair_mask(value)
    return jnp.concatenate([rows * first, rows * second], axis=0)


def one_pair(stacked):
    half = stacked.shape[0] // 2
    lane = iota((half, PAIR), 1)
    return jnp.where(lane < HEAD, stacked[:half], stacked[half:])


def kernel(
    n, rows, chunks,
    pad_ref, q_ref, k_ref, v_ref, g_ref,
    att_ref, qgrad_ref, kgrad_ref, vgrad_ref,
    kv, qg, own_qg, stats, bias, key_bias, expo_s, dprob_s,
    own_grad, suf_grad, down_out, down_in, up_out, up_in, chain_out, chain_in,
    load_sem, qg_send, qg_recv, suf_send, suf_recv, low_send, low_recv, high_send, high_recv,
    stat_send, stat_recv, down_send, down_recv, up_send, up_recv, chain_send, chain_recv,
):
    me = lax.axis_index("seq")
    last = n - 1
    below = lax.rem(me + n - 1, n)
    above = lax.rem(me + 1, n)
    has_below = me > 0
    has_above = me < last
    all_keys = rows + 2 * W + G
    own = slice(W, W + rows)
    low = slice(0, W)
    high = slice(W + rows, 2 * W + rows)
    suf = slice(2 * W + rows, all_keys)
    tail = slice(rows - G, rows)
    near = min(W, rows - G)

    def remote(src, dst, send, recv, target):
        return pltpu.make_async_remote_copy(
            src_ref=src, dst_ref=dst, send_sem=send, recv_sem=recv,
            device_id={"seq": target}, device_id_type=MESH,
        )

    def send_qg(c):
        return remote(qg.at[c], qg.at[c], qg_send.at[c], qg_recv.at[c], below)

    def send_suf(c):
        return remote(kv.at[c, :, suf], kv.at[c, :, suf], suf_send.at[c], suf_recv.at[c], below)

    def send_low(c):
        return remote(kv.at[c, :, own], kv.at[c, :, high], low_send.at[c], low_recv.at[c], below)

    def send_low_last(c):
        return remote(
            kv.at[c, :, W : W + near],
            kv.at[c, :, W + rows : W + rows + near],
            low_send.at[c], low_recv.at[c], below,
        )

    def send_up_last(c):
        return remote(
            up_out.at[c, :, :near], up_in.at[c, :, :near], up_send.at[c], up_recv.at[c], above
        )

    def send_high(c):
        return remote(kv.at[c, :, own], kv.at[c, :, low], high_send.at[c], high_recv.at[c], above)

    def send_down(c):
        return remote(down_out.at[c], down_in.at[c], down_send.at[c], down_recv.at[c], below)

    def send_up(c):
        return remote(up_out.at[c], up_in.at[c], up_send.at[c], up_recv.at[c], above)

    def send_chain(c):
        return remote(chain_out.at[c], chain_in.at[c], chain_send.at[c], chain_recv.at[c], above)

    def send_stats(k):
        return remote(
            stats.at[0], stats.at[k], stat_send.at[k], stat_recv.at[k], lax.rem(me + k, n)
        )

    barrier = pltpu.get_barrier_semaphore()
    for k in range(1, n):
        pl.semaphore_signal(
            barrier, inc=1, device_id={"seq": lax.rem(me + k, n)}, device_id_type=MESH
        )

    loads = []
    for c in range(chunks):
        columns = pl.ds(c * PAIR, PAIR)
        pieces = (
            (k_ref, kv.at[c, 0, own]),
            (v_ref, kv.at[c, 1, own]),
            (q_ref, own_qg.at[c, 0]),
            (g_ref, own_qg.at[c, 1]),
        )
        for k, (source, target) in enumerate(pieces):
            copy = pltpu.make_async_copy(source.at[0, :, columns], target, load_sem.at[c, k])
            copy.start()
            loads.append(copy)

    @pl.when(me == last)
    def _():
        for c in range(chunks):
            kv[c, :, high] = jnp.zeros((2, W, PAIR), bf16)

    @pl.when(me == last - 1)
    def _():
        for c in range(chunks):
            kv[c, :, W + rows + near : 2 * W + rows] = jnp.zeros((2, W - near, PAIR), bf16)

    @pl.when(me == 0)
    def _():
        for c in range(chunks):
            kv[c, :, low] = jnp.zeros((2, W, PAIR), bf16)

    for copy in loads:
        copy.wait()

    @pl.when(me == last)
    def _():
        for c in range(chunks):
            qg[c] = own_qg[c, :, tail]
            kv[c, :, suf] = kv[c, :, W + rows - G : W + rows]

    pl.semaphore_wait(barrier, n - 1)

    @pl.when(has_above)
    def _():
        for c in range(chunks):
            send_high(c).start()

    @pl.when(me == last)
    def _():
        for c in range(chunks):
            send_qg(c).start()
            send_suf(c).start()
        for c in range(chunks):
            send_low_last(c).start()

    @pl.when(has_above & has_below)
    def _():
        for c in range(AHEAD):
            send_low(c).start()

    suffix_start = rows * n - G
    valid_end = suffix_start - pad_ref[0]
    first_row = me * rows
    j = iota((all_keys, 2 * rows), 0)
    i = iota((all_keys, 2 * rows), 1)
    i = jnp.where(i >= rows, i - rows, i)
    key_pos = first_row - W + j
    apart = i - (j - W)
    within = (apart <= W) & (apart >= -W) & (key_pos >= 0) & (key_pos < valid_end)
    bias[...] = jnp.where(within | (j >= 2 * W + rows), 0.0, very_negative)
    own_pos = first_row + iota((rows, 2 * G), 0)
    key_bias[...] = jnp.where(
        (own_pos < valid_end) | (own_pos >= suffix_start), 0.0, very_negative
    )
    query_lane = iota((1, 2 * rows), 1)
    query_pos = first_row + jnp.where(query_lane >= rows, query_lane - rows, query_lane)
    row_live = jnp.where(query_pos < suffix_start, 1.0, 0.0)

    def forward_stats(c, carry):
        @pl.when(has_above)
        def _():
            send_qg(c).wait_recv()

            @pl.when(has_below)
            def _():
                send_qg(c).start()

            send_suf(c).wait_recv()

            @pl.when(has_below)
            def _():
                send_suf(c).start()

        query_two = two_heads(qg[c, 0], scale)
        grad_two = two_heads(qg[c, 1], 1.0)
        scores = dot_nt(kv[c, 0, own], query_two) + key_bias[...]
        largest = jnp.max(scores, axis=0, keepdims=True)
        expo = jnp.exp(scores - largest)
        dprob = dot_nt(kv[c, 1, own], grad_two)
        total = jnp.sum(expo, axis=0, keepdims=True)
        weighted = jnp.sum(expo * dprob, axis=0, keepdims=True)
        expo_s[c] = expo
        dprob_s[c] = dprob
        row = iota((8, 2 * G), 0)
        stats[0, c] = jnp.where(row == 0, largest, jnp.where(row == 1, total, weighted))
        return carry

    lax.fori_loop(0, chunks, forward_stats, 0)
    for k in range(1, n):
        send_stats(k).start()

    @pl.when(has_above & has_below)
    def _():
        for c in range(AHEAD, chunks):
            send_low(c).start()

    def band(c):
        @pl.when(has_below)
        def _():
            send_high(c).wait_recv()

        @pl.when(me < last - 1)
        def _():
            send_low(c).wait_recv()

        @pl.when(me == last - 1)
        def _():
            send_low_last(c).wait_recv()

        columns = pl.ds(pl.multiple_of(c * PAIR, PAIR), PAIR)
        query_two = two_heads(own_qg[c, 0], scale)
        grad_two = two_heads(own_qg[c, 1], 1.0)
        keys = kv[c, 0]
        values = kv[c, 1]
        scores = dot_nt(keys, query_two) + bias[...]
        largest = jnp.max(scores, axis=0, keepdims=True)
        expo = jnp.exp(scores - largest)
        total = jnp.sum(expo, axis=0, keepdims=True)
        dprob = dot_nt(values, grad_two)
        inverse = 1.0 / total
        delta = jnp.sum(expo * dprob, axis=0, keepdims=True) * inverse
        probs = expo * (inverse * row_live)
        probs_low = probs.astype(bf16)
        dscore = (probs * (dprob - delta)).astype(bf16)
        att_ref[:, columns] = one_pair(dot_tn(probs_low, values)).astype(bf16)
        qgrad_ref[:, columns] = (one_pair(dot_tn(dscore, keys)) * scale).astype(bf16)
        key_all = dot_nn(dscore, query_two)
        value_all = dot_nn(probs_low, grad_two)
        down_out[c, 0] = key_all[low].astype(bf16)
        down_out[c, 1] = value_all[low].astype(bf16)
        up_out[c, 0] = key_all[high].astype(bf16)
        up_out[c, 1] = value_all[high].astype(bf16)

        own_grad[c, 0] = key_all[own]
        own_grad[c, 1] = value_all[own]
        suf_grad[c, 0] = key_all[suf]
        suf_grad[c, 1] = value_all[suf]

    def finish(c):
        columns = pl.ds(pl.multiple_of(c * PAIR, PAIR), PAIR)
        parts = [stats[k, c] for k in range(n)]
        top = parts[0][0:1]
        for part in parts[1:]:
            top = jnp.maximum(top, part[0:1])
        factors = [jnp.exp(part[0:1] - top) for part in parts]
        total = sum(factor * part[1:2] for factor, part in zip(factors, parts))
        weighted = sum(factor * part[2:3] for factor, part in zip(factors, parts))
        inverse = 1.0 / total
        delta = weighted * inverse
        probs = expo_s[c] * (factors[0] * inverse)
        probs_low = probs.astype(bf16)
        dscore = (probs * (dprob_s[c] - delta)).astype(bf16)
        query_two = two_heads(qg[c, 0], scale)
        grad_two = two_heads(qg[c, 1], 1.0)
        att_part = one_pair(dot_tn(probs_low, kv[c, 1, own]))
        query_part = one_pair(dot_tn(dscore, kv[c, 0, own])) * scale
        suf_key = suf_grad[c, 0]
        suf_value = suf_grad[c, 1]
        key_sum = own_grad[c, 0] + dot_nn(dscore, query_two)
        value_sum = own_grad[c, 1] + dot_nn(probs_low, grad_two)

        @pl.when(me == 0)
        def _():
            chain_out[c, 0] = att_part.astype(bf16)
            chain_out[c, 1] = query_part.astype(bf16)
            chain_out[c, 2] = suf_key.astype(bf16)
            chain_out[c, 3] = suf_value.astype(bf16)

        own_grad[c, 0] = key_sum
        own_grad[c, 1] = value_sum

        @pl.when(has_below)
        def _():
            send_chain(c).wait_recv()
            att_sum = att_part + chain_in[c, 0].astype(f32)
            query_sum = query_part + chain_in[c, 1].astype(f32)
            key_suf = suf_key + chain_in[c, 2].astype(f32)
            value_suf = suf_value + chain_in[c, 3].astype(f32)

            @pl.when(has_above)
            def _():
                chain_out[c, 0] = att_sum.astype(bf16)
                chain_out[c, 1] = query_sum.astype(bf16)
                chain_out[c, 2] = key_suf.astype(bf16)
                chain_out[c, 3] = value_suf.astype(bf16)

            @pl.when(me == last)
            def _():
                att_ref[tail, columns] = att_sum.astype(bf16)
                qgrad_ref[tail, columns] = query_sum.astype(bf16)
                own_grad[c, 0, tail] = own_grad[c, 0, tail] + key_suf
                own_grad[c, 1, tail] = own_grad[c, 1, tail] + value_suf

        @pl.when(has_above)
        def _():
            send_chain(c).start()

    lag = jnp.minimum(CHAIN_LAG * me, chunks)

    def step(t, carry):
        @pl.when(t < chunks)
        def _():
            band(t)

            @pl.when(me == last)
            def _():
                send_low_last(t).wait_send()

        @pl.when(t == lag)
        def _():
            for k in range(1, n):
                send_stats(k).wait_recv()

        @pl.when((t >= lag) & (t < lag + chunks))
        def _():
            finish(t - lag)

        @pl.when((t >= UP_LAG) & (t < UP_LAG + chunks))
        def _():
            @pl.when(me < last - 1)
            def _():
                send_up(t - UP_LAG).start()

            @pl.when(me == last - 1)
            def _():
                send_up_last(t - UP_LAG).start()

        @pl.when((t >= DOWN_LAG) & (t < DOWN_LAG + chunks) & has_below)
        def _():
            send_down(t - DOWN_LAG).start()

        return carry

    lax.fori_loop(0, 2 * chunks, step, 0)

    def combine(c, carry):
        columns = pl.ds(pl.multiple_of(c * PAIR, PAIR), PAIR)

        @pl.when(has_below)
        def _():
            @pl.when(me < last)
            def _():
                send_up(c).wait_recv()
                own_grad[c, :, 0:W] = own_grad[c, :, 0:W] + up_in[c].astype(f32)

            @pl.when(me == last)
            def _():
                send_up_last(c).wait_recv()
                own_grad[c, :, 0:near] = own_grad[c, :, 0:near] + up_in[c, :, 0:near].astype(f32)

        @pl.when(has_above)
        def _():
            send_down(c).wait_recv()
            own_grad[c, :, rows - W : rows] = own_grad[c, :, rows - W : rows] + down_in[
                c
            ].astype(f32)

        kgrad_ref[:, columns] = own_grad[c, 0].astype(bf16)
        vgrad_ref[:, columns] = own_grad[c, 1].astype(bf16)
        return carry

    lax.fori_loop(0, chunks, combine, 0)

    def drain(c, carry):
        @pl.when(has_below)
        def _():
            send_qg(c).wait_send()
            send_suf(c).wait_send()

            @pl.when(has_above)
            def _():
                send_low(c).wait_send()

            send_down(c).wait_send()

        @pl.when(has_above)
        def _():
            send_high(c).wait_send()
            send_chain(c).wait_send()

        @pl.when(me < last - 1)
        def _():
            send_up(c).wait_send()

        @pl.when(me == last - 1)
        def _():
            send_up_last(c).wait_send()

        return carry

    lax.fori_loop(0, chunks, drain, 0)
    for k in range(1, n):
        send_stats(k).wait_send()


def per_device(n, query_vectors, key_vectors, value_vectors, out_grad, pad_length):
    rows, features = query_vectors.shape[1:]
    chunks = features // PAIR
    all_keys = rows + 2 * W + G
    vmem = pl.BlockSpec(memory_space=pltpu.VMEM)
    smem = pl.BlockSpec(memory_space=pltpu.SMEM)
    out = jax.ShapeDtypeStruct((rows, features), bf16)
    dma = pltpu.SemaphoreType.DMA
    outs = pl.pallas_call(
        functools.partial(kernel, n, rows, chunks),
        out_shape=(out,) * 4,
        in_specs=[smem] + [pl.BlockSpec(memory_space=pl.ANY)] * 4,
        out_specs=(vmem,) * 4,
        scratch_shapes=[
            pltpu.VMEM((chunks, 2, all_keys, PAIR), bf16),
            pltpu.VMEM((chunks, 2, G, PAIR), bf16),
            pltpu.VMEM((chunks, 2, rows, PAIR), bf16),
            pltpu.VMEM((n, chunks, 8, 2 * G), f32),
            pltpu.VMEM((all_keys, 2 * rows), f32),
            pltpu.VMEM((rows, 2 * G), f32),
            pltpu.VMEM((chunks, rows, 2 * G), f32),
            pltpu.VMEM((chunks, rows, 2 * G), f32),
            pltpu.VMEM((chunks, 2, rows, PAIR), f32),
            pltpu.VMEM((chunks, 2, G, PAIR), f32),
            pltpu.VMEM((chunks, 2, W, PAIR), bf16),
            pltpu.VMEM((chunks, 2, W, PAIR), bf16),
            pltpu.VMEM((chunks, 2, W, PAIR), bf16),
            pltpu.VMEM((chunks, 2, W, PAIR), bf16),
            pltpu.VMEM((chunks, 4, G, PAIR), bf16),
            pltpu.VMEM((chunks, 4, G, PAIR), bf16),
        ]
        + [dma((chunks, 4))]
        + [dma((chunks,))] * 8
        + [dma((n,))] * 2
        + [dma((chunks,))] * 6,
        compiler_params=pltpu.CompilerParams(
            collective_id=0, has_side_effects=True, vmem_limit_bytes=48 << 20
        ),
    )(pad_length, query_vectors, key_vectors, value_vectors, out_grad)
    return tuple(array[None] for array in outs)


def solution(mesh):
    rows = P(("group", "doc"), "seq", None)
    return jax.shard_map(
        functools.partial(per_device, mesh.shape["seq"]),
        mesh=mesh,
        in_specs=(rows, rows, rows, rows, P(("group", "doc"))),
        out_specs=(rows,) * 4,
        check_vma=False,
    )
```

```python
import functools
import math

import jax
import jax.numpy as jnp
from jax import lax
from jax.experimental import pallas as pl
from jax.experimental.pallas import tpu as pltpu
from jax.sharding import PartitionSpec as P

D = 1024
H = 16
W = 128
G = 64
HEAD = D // H
PAIR = 2 * HEAD
AHEAD = 2
CHAIN_LAG = 3
UP_LAG = 2
DOWN_LAG = 2

MESH = pl.DeviceIdType.MESH
very_negative = -1e30
scale = 1.0 / math.sqrt(HEAD)
f32 = jnp.float32
bf16 = jnp.bfloat16


def dot_nt(a, b):
    return lax.dot_general(a, b, (((1,), (1,)), ((), ())), preferred_element_type=f32)


def dot_nn(a, b):
    return lax.dot_general(a, b, (((1,), (0,)), ((), ())), preferred_element_type=f32)


def dot_tn(a, b):
    return lax.dot_general(a, b, (((0,), (0,)), ((), ())), preferred_element_type=f32)


def iota(shape, dim):
    return lax.broadcasted_iota(jnp.int32, shape, dim)


def pair_mask(value):
    lane = iota((1, PAIR), 1)
    first = jnp.where(lane < HEAD, value, 0.0).astype(bf16)
    second = jnp.where(lane < HEAD, 0.0, value).astype(bf16)
    return first, second


def two_heads(rows, value):
    first, second = pair_mask(value)
    return jnp.concatenate([rows * first, rows * second], axis=0)


def one_pair(stacked):
    half = stacked.shape[0] // 2
    lane = iota((half, PAIR), 1)
    return jnp.where(lane < HEAD, stacked[:half], stacked[half:])


def kernel(
    n, rows, chunks,
    pad_ref, q_ref, k_ref, v_ref, g_ref,
    att_ref, qgrad_ref, kgrad_ref, vgrad_ref,
    kv, qg, own_qg, stats, bias, key_bias, expo_s, dprob_s,
    own_grad, suf_grad, down_out, down_in, up_out, up_in, chain_out, chain_in,
    load_sem, qg_send, qg_recv, suf_send, suf_recv, low_send, low_recv, high_send, high_recv,
    stat_send, stat_recv, down_send, down_recv, up_send, up_recv, chain_send, chain_recv,
):
    me = lax.axis_index("seq")
    last = n - 1
    below = lax.rem(me + n - 1, n)
    above = lax.rem(me + 1, n)
    has_below = me > 0
    has_above = me < last
    all_keys = rows + 2 * W + G
    own = slice(W, W + rows)
    low = slice(0, W)
    high = slice(W + rows, 2 * W + rows)
    suf = slice(2 * W + rows, all_keys)
    tail = slice(rows - G, rows)
    near = min(W, rows - G)

    def remote(src, dst, send, recv, target):
        return pltpu.make_async_remote_copy(
            src_ref=src, dst_ref=dst, send_sem=send, recv_sem=recv,
            device_id={"seq": target}, device_id_type=MESH,
        )

    def send_qg(c):
        return remote(qg.at[c], qg.at[c], qg_send.at[c], qg_recv.at[c], below)

    def send_suf(c):
        return remote(kv.at[c, :, suf], kv.at[c, :, suf], suf_send.at[c], suf_recv.at[c], below)

    def send_low(c):
        return remote(kv.at[c, :, own], kv.at[c, :, high], low_send.at[c], low_recv.at[c], below)

    def send_low_last(c):
        return remote(
            kv.at[c, :, W : W + near],
            kv.at[c, :, W + rows : W + rows + near],
            low_send.at[c], low_recv.at[c], below,
        )

    def send_up_last(c):
        return remote(
            up_out.at[c, :, :near], up_in.at[c, :, :near], up_send.at[c], up_recv.at[c], above
        )

    def send_high(c):
        return remote(kv.at[c, :, own], kv.at[c, :, low], high_send.at[c], high_recv.at[c], above)

    def send_down(c):
        return remote(down_out.at[c], down_in.at[c], down_send.at[c], down_recv.at[c], below)

    def send_up(c):
        return remote(up_out.at[c], up_in.at[c], up_send.at[c], up_recv.at[c], above)

    def send_chain(c):
        return remote(chain_out.at[c], chain_in.at[c], chain_send.at[c], chain_recv.at[c], above)

    def send_stats(k):
        return remote(
            stats.at[0], stats.at[k], stat_send.at[k], stat_recv.at[k], lax.rem(me + k, n)
        )

    barrier = pltpu.get_barrier_semaphore()
    for k in range(1, n):
        pl.semaphore_signal(
            barrier, inc=1, device_id={"seq": lax.rem(me + k, n)}, device_id_type=MESH
        )

    loads = []
    for c in range(chunks):
        columns = pl.ds(c * PAIR, PAIR)
        pieces = (
            (k_ref, kv.at[c, 0, own]),
            (v_ref, kv.at[c, 1, own]),
            (q_ref, own_qg.at[c, 0]),
            (g_ref, own_qg.at[c, 1]),
        )
        for k, (source, target) in enumerate(pieces):
            copy = pltpu.make_async_copy(source.at[0, :, columns], target, load_sem.at[c, k])
            copy.start()
            loads.append(copy)

    @pl.when(me == last)
    def _():
        for c in range(chunks):
            kv[c, :, high] = jnp.zeros((2, W, PAIR), bf16)

    @pl.when(me == last - 1)
    def _():
        for c in range(chunks):
            kv[c, :, W + rows + near : 2 * W + rows] = jnp.zeros((2, W - near, PAIR), bf16)

    @pl.when(me == 0)
    def _():
        for c in range(chunks):
            kv[c, :, low] = jnp.zeros((2, W, PAIR), bf16)

    for copy in loads:
        copy.wait()

    @pl.when(me == last)
    def _():
        for c in range(chunks):
            qg[c] = own_qg[c, :, tail]
            kv[c, :, suf] = kv[c, :, W + rows - G : W + rows]

    pl.semaphore_wait(barrier, n - 1)

    @pl.when(has_above)
    def _():
        for c in range(chunks):
            send_high(c).start()

    @pl.when(me == last)
    def _():
        for c in range(chunks):
            send_qg(c).start()
            send_suf(c).start()
        for c in range(chunks):
            send_low_last(c).start()

    @pl.when(has_above & has_below)
    def _():
        for c in range(AHEAD):
            send_low(c).start()

    suffix_start = rows * n - G
    valid_end = suffix_start - pad_ref[0]
    first_row = me * rows
    j = iota((all_keys, 2 * rows), 0)
    i = iota((all_keys, 2 * rows), 1)
    i = jnp.where(i >= rows, i - rows, i)
    key_pos = first_row - W + j
    apart = i - (j - W)
    within = (apart <= W) & (apart >= -W) & (key_pos >= 0) & (key_pos < valid_end)
    bias[...] = jnp.where(within | (j >= 2 * W + rows), 0.0, very_negative)
    own_pos = first_row + iota((rows, 2 * G), 0)
    key_bias[...] = jnp.where(
        (own_pos < valid_end) | (own_pos >= suffix_start), 0.0, very_negative
    )
    query_lane = iota((1, 2 * rows), 1)
    query_pos = first_row + jnp.where(query_lane >= rows, query_lane - rows, query_lane)
    row_live = jnp.where(query_pos < suffix_start, 1.0, 0.0)

    def forward_stats(c, carry):
        @pl.when(has_above)
        def _():
            send_qg(c).wait_recv()

            @pl.when(has_below)
            def _():
                send_qg(c).start()

            send_suf(c).wait_recv()

            @pl.when(has_below)
            def _():
                send_suf(c).start()

        query_two = two_heads(qg[c, 0], scale)
        grad_two = two_heads(qg[c, 1], 1.0)
        scores = dot_nt(kv[c, 0, own], query_two) + key_bias[...]
        largest = jnp.max(scores, axis=0, keepdims=True)
        expo = jnp.exp(scores - largest)
        dprob = dot_nt(kv[c, 1, own], grad_two)
        total = jnp.sum(expo, axis=0, keepdims=True)
        weighted = jnp.sum(expo * dprob, axis=0, keepdims=True)
        expo_s[c] = expo
        dprob_s[c] = dprob
        row = iota((8, 2 * G), 0)
        stats[0, c] = jnp.where(row == 0, largest, jnp.where(row == 1, total, weighted))
        return carry

    lax.fori_loop(0, chunks, forward_stats, 0)
    for k in range(1, n):
        send_stats(k).start()

    @pl.when(has_above & has_below)
    def _():
        for c in range(AHEAD, chunks):
            send_low(c).start()

    def band(c):
        @pl.when(has_below)
        def _():
            send_high(c).wait_recv()

        @pl.when(me < last - 1)
        def _():
            send_low(c).wait_recv()

        @pl.when(me == last - 1)
        def _():
            send_low_last(c).wait_recv()

        columns = pl.ds(pl.multiple_of(c * PAIR, PAIR), PAIR)
        query_two = two_heads(own_qg[c, 0], scale)
        grad_two = two_heads(own_qg[c, 1], 1.0)
        keys = kv[c, 0]
        values = kv[c, 1]
        scores = dot_nt(keys, query_two) + bias[...]
        largest = jnp.max(scores, axis=0, keepdims=True)
        expo = jnp.exp(scores - largest)
        total = jnp.sum(expo, axis=0, keepdims=True)
        dprob = dot_nt(values, grad_two)
        inverse = 1.0 / total
        delta = jnp.sum(expo * dprob, axis=0, keepdims=True) * inverse
        probs = expo * (inverse * row_live)
        probs_low = probs.astype(bf16)
        dscore = (probs * (dprob - delta)).astype(bf16)
        att_ref[:, columns] = one_pair(dot_tn(probs_low, values)).astype(bf16)
        qgrad_ref[:, columns] = (one_pair(dot_tn(dscore, keys)) * scale).astype(bf16)
        key_all = dot_nn(dscore, query_two)
        value_all = dot_nn(probs_low, grad_two)
        down_out[c, 0] = key_all[low].astype(bf16)
        down_out[c, 1] = value_all[low].astype(bf16)
        up_out[c, 0] = key_all[high].astype(bf16)
        up_out[c, 1] = value_all[high].astype(bf16)

        own_grad[c, 0] = key_all[own]
        own_grad[c, 1] = value_all[own]
        suf_grad[c, 0] = key_all[suf]
        suf_grad[c, 1] = value_all[suf]

    def finish(c):
        columns = pl.ds(pl.multiple_of(c * PAIR, PAIR), PAIR)
        parts = [stats[k, c] for k in range(n)]
        top = parts[0][0:1]
        for part in parts[1:]:
            top = jnp.maximum(top, part[0:1])
        factors = [jnp.exp(part[0:1] - top) for part in parts]
        total = sum(factor * part[1:2] for factor, part in zip(factors, parts))
        weighted = sum(factor * part[2:3] for factor, part in zip(factors, parts))
        inverse = 1.0 / total
        delta = weighted * inverse
        probs = expo_s[c] * (factors[0] * inverse)
        probs_low = probs.astype(bf16)
        dscore = (probs * (dprob_s[c] - delta)).astype(bf16)
        query_two = two_heads(qg[c, 0], scale)
        grad_two = two_heads(qg[c, 1], 1.0)
        att_part = one_pair(dot_tn(probs_low, kv[c, 1, own]))
        query_part = one_pair(dot_tn(dscore, kv[c, 0, own])) * scale
        suf_key = suf_grad[c, 0]
        suf_value = suf_grad[c, 1]
        key_sum = own_grad[c, 0] + dot_nn(dscore, query_two)
        value_sum = own_grad[c, 1] + dot_nn(probs_low, grad_two)

        @pl.when(me == 0)
        def _():
            chain_out[c, 0] = att_part.astype(bf16)
            chain_out[c, 1] = query_part.astype(bf16)
            chain_out[c, 2] = suf_key.astype(bf16)
            chain_out[c, 3] = suf_value.astype(bf16)

        own_grad[c, 0] = key_sum
        own_grad[c, 1] = value_sum

        @pl.when(has_below)
        def _():
            send_chain(c).wait_recv()
            att_sum = att_part + chain_in[c, 0].astype(f32)
            query_sum = query_part + chain_in[c, 1].astype(f32)
            key_suf = suf_key + chain_in[c, 2].astype(f32)
            value_suf = suf_value + chain_in[c, 3].astype(f32)

            @pl.when(has_above)
            def _():
                chain_out[c, 0] = att_sum.astype(bf16)
                chain_out[c, 1] = query_sum.astype(bf16)
                chain_out[c, 2] = key_suf.astype(bf16)
                chain_out[c, 3] = value_suf.astype(bf16)

            @pl.when(me == last)
            def _():
                att_ref[tail, columns] = att_sum.astype(bf16)
                qgrad_ref[tail, columns] = query_sum.astype(bf16)
                own_grad[c, 0, tail] = own_grad[c, 0, tail] + key_suf
                own_grad[c, 1, tail] = own_grad[c, 1, tail] + value_suf

        @pl.when(has_above)
        def _():
            send_chain(c).start()

    def combine(c):
        columns = pl.ds(pl.multiple_of(c * PAIR, PAIR), PAIR)

        @pl.when(has_below)
        def _():
            @pl.when(me < last)
            def _():
                send_up(c).wait_recv()
                own_grad[c, :, 0:W] = own_grad[c, :, 0:W] + up_in[c].astype(f32)

            @pl.when(me == last)
            def _():
                send_up_last(c).wait_recv()
                own_grad[c, :, 0:near] = own_grad[c, :, 0:near] + up_in[c, :, 0:near].astype(f32)

        @pl.when(has_above)
        def _():
            send_down(c).wait_recv()
            own_grad[c, :, rows - W : rows] = own_grad[c, :, rows - W : rows] + down_in[
                c
            ].astype(f32)

        kgrad_ref[:, columns] = own_grad[c, 0].astype(bf16)
        vgrad_ref[:, columns] = own_grad[c, 1].astype(bf16)

    lag = jnp.minimum(CHAIN_LAG * me, chunks)

    def step(t, carry):
        @pl.when(t < chunks)
        def _():
            band(t)

            @pl.when(me == last)
            def _():
                send_low_last(t).wait_send()

        @pl.when(t == lag)
        def _():
            for k in range(1, n):
                send_stats(k).wait_recv()

        @pl.when((t >= lag) & (t < lag + chunks))
        def _():
            finish(t - lag)

        @pl.when((t >= UP_LAG) & (t < UP_LAG + chunks))
        def _():
            @pl.when(me < last - 1)
            def _():
                send_up(t - UP_LAG).start()

            @pl.when(me == last - 1)
            def _():
                send_up_last(t - UP_LAG).start()

        @pl.when((t >= DOWN_LAG) & (t < DOWN_LAG + chunks) & has_below)
        def _():
            send_down(t - DOWN_LAG).start()

        @pl.when(t >= chunks)
        def _():
            combine(t - chunks)

        return carry

    lax.fori_loop(0, 2 * chunks, step, 0)

    def drain(c, carry):
        @pl.when(has_below)
        def _():
            send_qg(c).wait_send()
            send_suf(c).wait_send()

            @pl.when(has_above)
            def _():
                send_low(c).wait_send()

            send_down(c).wait_send()

        @pl.when(has_above)
        def _():
            send_high(c).wait_send()
            send_chain(c).wait_send()

        @pl.when(me < last - 1)
        def _():
            send_up(c).wait_send()

        @pl.when(me == last - 1)
        def _():
            send_up_last(c).wait_send()

        return carry

    lax.fori_loop(0, chunks, drain, 0)
    for k in range(1, n):
        send_stats(k).wait_send()


def spill(*refs):
    sems = refs[8]
    copies = [
        pltpu.make_async_copy(refs[k], refs[4 + k].at[0], sems.at[k]) for k in range(4)
    ]
    for copy in copies:
        copy.start()
    for copy in copies:
        copy.wait()


def per_device(n, query_vectors, key_vectors, value_vectors, out_grad, pad_length):
    rows, features = query_vectors.shape[1:]
    chunks = features // PAIR
    all_keys = rows + 2 * W + G
    vmem = pl.BlockSpec(memory_space=pltpu.VMEM)
    smem = pl.BlockSpec(memory_space=pltpu.SMEM)
    out = jax.ShapeDtypeStruct((rows, features), bf16)
    dma = pltpu.SemaphoreType.DMA
    outs = pl.pallas_call(
        functools.partial(kernel, n, rows, chunks),
        out_shape=(out,) * 4,
        in_specs=[smem] + [pl.BlockSpec(memory_space=pltpu.HBM)] * 4,
        out_specs=(vmem,) * 4,
        scratch_shapes=[
            pltpu.VMEM((chunks, 2, all_keys, PAIR), bf16),
            pltpu.VMEM((chunks, 2, G, PAIR), bf16),
            pltpu.VMEM((chunks, 2, rows, PAIR), bf16),
            pltpu.VMEM((n, chunks, 8, 2 * G), f32),
            pltpu.VMEM((all_keys, 2 * rows), f32),
            pltpu.VMEM((rows, 2 * G), f32),
            pltpu.VMEM((chunks, rows, 2 * G), f32),
            pltpu.VMEM((chunks, rows, 2 * G), f32),
            pltpu.VMEM((chunks, 2, rows, PAIR), f32),
            pltpu.VMEM((chunks, 2, G, PAIR), f32),
            pltpu.VMEM((chunks, 2, W, PAIR), bf16),
            pltpu.VMEM((chunks, 2, W, PAIR), bf16),
            pltpu.VMEM((chunks, 2, W, PAIR), bf16),
            pltpu.VMEM((chunks, 2, W, PAIR), bf16),
            pltpu.VMEM((chunks, 4, G, PAIR), bf16),
            pltpu.VMEM((chunks, 4, G, PAIR), bf16),
        ]
        + [dma((chunks, 4))]
        + [dma((chunks,))] * 8
        + [dma((n,))] * 2
        + [dma((chunks,))] * 6,
        compiler_params=pltpu.CompilerParams(
            collective_id=0, has_side_effects=True, vmem_limit_bytes=63 << 20
        ),
    )(pad_length, query_vectors, key_vectors, value_vectors, out_grad)
    anywhere = pl.BlockSpec(memory_space=pl.ANY)
    return pl.pallas_call(
        spill,
        out_shape=(jax.ShapeDtypeStruct((1, rows, features), bf16),) * 4,
        in_specs=[vmem] * 4,
        out_specs=(anywhere,) * 4,
        scratch_shapes=[dma((4,))],
    )(*outs)


def solution(mesh):
    rows = P(("group", "doc"), "seq", None)
    return jax.shard_map(
        functools.partial(per_device, mesh.shape["seq"]),
        mesh=mesh,
        in_specs=(rows, rows, rows, rows, P(("group", "doc"))),
        out_specs=(rows,) * 4,
        check_vma=False,
    )
```
